32 devices in a mesh: txt: 4 (over z), aud: 8 (over y, x, core).
Axes of the slice: x: 2, y: 2, z: 4, core: 2. Of those that a mesh axis runs over, the one named last changes fastest.
Arguments:
- images: float32 [8192, 1024], P(('txt', 'aud')), may hold values from -2 to 2
- texts: float32 [64, 1024], P('txt'), may hold values from -2 to 2
- audio: float32 [32, 1024], P('aud'), may hold values from -2 to 2
- pos_text: int32 [8192], P(('txt', 'aud')), may hold values from 0 to 63
- pos_audio: int32 [8192], P(('txt', 'aud')), may hold values from 0 to 11
- logit_scale: float32 [1], replicated, may hold values from 1 to 4
- logit_bias: float32 [1], replicated, may hold values from -3 to -1
Outputs:
- grad_images: float32 [8192, 1024], P(('txt', 'aud'))
- grad_texts: float32 [64, 1024], P('txt')
- grad_audio: float32 [32, 1024], P('aud')
The draws below stay inside these ranges and needn't reach their ends.
All inputs are finite; a program needn't handle non-finite values.
Results may differ from the reference program's by a relative error of at most 0.0044.
Values sent between devices are 32-bit elements; how exact they have to be, the bound alone decides.
A program may use at most 64 MiB of HBM per device.

```python
import math
import jax
import jax.numpy as jnp
from jax import lax

D = 1024
I_DEV = 256
AB = 4
HOPS = 2
IMAGES = 8192
TEXTS = 64
AUDIO = 32
N_TXT = 4
N_AUD = 8


def set_ends(result, rng, least, high):
    dims = result.shape
    spot = [jax.random.randint(jax.random.fold_in(rng, axis), (), 0, dims[axis]) for axis in range(len(dims))]
    result = result.at[tuple(spot)].set(least)
    longest = dims.index(max(dims))
    spot[longest] = (spot[longest] + 1) % dims[longest]
    return result.at[tuple(spot)].set(high)


def levels(rng, dims, shards, low, top_value):
    factor_of, own = 1.0, jax.random.fold_in(rng, 6)
    for dim, shards_of in shards:
        heights = jnp.exp(jax.random.uniform(jax.random.fold_in(own, dim), (shards_of,), jnp.float32, low / len(shards), top_value / len(shards)))
        factor_of = factor_of * jnp.repeat(heights, dims[dim] // shards_of).reshape([-1 if axis == dim else 1 for axis in range(len(dims))])
    return factor_of


def scatter_about(own_key, dims, deviation, reach, shards=(), kind=jnp.bfloat16):
    array = deviation * jax.random.normal(own_key, dims, jnp.float32)
    if shards:
        array = array * levels(own_key, dims, shards, -0.22, 0.18)
    return jnp.clip(array, -reach, reach).astype(kind)


def setup_inputs(seed: int = 0) -> dict:
    key_list = jax.random.split(jax.random.key(seed), 8)
    return {
        "images": scatter_about(key_list[0], (IMAGES, D), 0.3, 2.0, ((0, 32),), jnp.float32),
        "texts": scatter_about(key_list[1], (TEXTS, D), 0.3, 2.0, ((0, 4),), jnp.float32),
        "audio": scatter_about(key_list[2], (AUDIO, D), 0.3, 2.0, ((0, 8),), jnp.float32),
        "pos_text": set_ends(jax.random.randint(key_list[3], (IMAGES,), 0, TEXTS), jax.random.fold_in(key_list[3], 1), 0, TEXTS - 1).astype(jnp.int32),
        "pos_audio": set_ends(jax.random.randint(key_list[4], (IMAGES,), 0, (HOPS + 1) * AB), jax.random.fold_in(key_list[4], 1), 0, ((HOPS + 1) * AB) - 1).astype(jnp.int32),
        "logit_scale": jnp.clip(jnp.exp(jax.random.uniform(key_list[5], (1,), jnp.float32, math.log(1.0), math.log(4.0))), 1.0, 4.0),
        "logit_bias": jnp.clip(jax.random.uniform(key_list[6], (1,), jnp.float32, -3.0, -1.0), -3.0, -1.0),
    }


def block_terms(image_half, text_piece, window, first_row, pos_text, pos_audio, temper, offset):
    row_count = text_piece.shape[0]
    slot_count = window.shape[0]
    products = (text_piece[:, None, :] * window[None, :, :]).reshape(row_count * slot_count, -1).astype(jnp.bfloat16)
    logits = temper * lax.dot_general(image_half, products, (((1,), (1,)), ((), ())), preferred_element_type=jnp.float32) + offset
    columns = jnp.arange(row_count * slot_count, dtype=jnp.int32)
    text_of = first_row + columns // slot_count
    slot_of = columns % slot_count
    positive = (text_of[None, :] == pos_text[:, None]) & (slot_of[None, :] == pos_audio[:, None])
    slope = ((jax.nn.sigmoid(logits) - positive.astype(jnp.float32)) * temper).astype(jnp.bfloat16)
    grad_image = jnp.dot(slope, products, preferred_element_type=jnp.float32)
    grad_prod = lax.dot_general(slope, image_half, (((0,), (0,)), ((), ())), preferred_element_type=jnp.float32)
    grad_prod = grad_prod.reshape(row_count, slot_count, -1)
    grad_piece = jnp.sum(grad_prod * window[None, :, :], axis=1)
    grad_window = jnp.sum(grad_prod * text_piece[:, None, :], axis=0)
    return grad_image, grad_piece, grad_window


def reference(images, texts, audio, pos_text, pos_audio, logit_scale, logit_bias):
    temper = logit_scale[0]
    offset = logit_bias[0]
    audio_blocks = audio.reshape(N_AUD, AB, D)

    def visit(carry, block):
        text_acc, audio_acc = carry
        column = block % N_AUD
        picks = ((column + jnp.arange(HOPS + 1, dtype=jnp.int32)) % N_AUD).astype(jnp.int32)
        window = jnp.take(audio_blocks, picks, axis=0).reshape((HOPS + 1) * AB, D)
        first = (block * I_DEV).astype(jnp.int32)
        image_rows = lax.dynamic_slice_in_dim(images, first, I_DEV, 0)
        text_pos = lax.dynamic_slice_in_dim(pos_text, first, I_DEV, 0)
        audio_pos = lax.dynamic_slice_in_dim(pos_audio, first, I_DEV, 0)
        grad_image, grad_piece, grad_window = block_terms(image_rows.astype(jnp.bfloat16), texts, window, jnp.int32(0), text_pos, audio_pos, temper, offset)
        audio_acc = audio_acc.at[picks].add(grad_window.reshape(HOPS + 1, AB, D))
        return (text_acc + grad_piece, audio_acc), grad_image

    start_state = (jnp.zeros((TEXTS, D), jnp.float32), jnp.zeros((N_AUD, AB, D), jnp.float32))
    blocks = jnp.arange(N_TXT * N_AUD, dtype=jnp.int32)
    (grad_texts, grad_audio), grad_images = lax.scan(visit, start_state, blocks)
    return grad_images.reshape(IMAGES, D), grad_texts, grad_audio.reshape(AUDIO, D)
```

```python
import functools
import jax
import jax.numpy as jnp
from jax import lax
from jax.experimental import pallas as pl
from jax.experimental.pallas import tpu as pltpu
from jax.sharding import PartitionSpec as P

HOPS = 2
MESH = pl.DeviceIdType.MESH
LANES = 128


def each(count, body, start=0):
    if count - start <= 8:
        for i in range(start, count):
            body(i)
    else:
        lax.fori_loop(start, count, lambda i, c: (body(i), c)[1], 0)


def kernel(
    n_txt,
    n_aud,
    images,
    texts,
    audio,
    pos_text,
    pos_audio,
    scale,
    bias,
    grad_images,
    grad_texts,
    grad_audio,
    image_buf,
    image_half,
    text_all,
    window,
    products,
    slopes,
    window_acc,
    text_out,
    text_in,
    text_sum,
    text_z,
    piece,
    pieces,
    home_out,
    home_in,
    audio_sum,
    audio_z,
    result_buf,
    load_sem,
    gather_send,
    gather_recv,
    relay_send,
    relay_recv,
    audio_send,
    audio_recv,
    scatter_send,
    scatter_recv,
    home_send,
    home_recv,
    z_send,
    z_recv,
    za_send,
    za_recv,
    spread_send,
    spread_recv,
    store_sem,
):
    t = lax.axis_index("txt")
    a = lax.axis_index("aud")
    text_rows, width = texts.shape
    half_rows = text_rows // 2
    block = audio.shape[0]
    slots = (HOPS + 1) * block
    cols = slots * text_rows
    chunk_rows, chunk_cols = piece.shape
    n_col = width // chunk_cols
    half = lax.rem(a, 2)
    other = 1 - half
    partner = a + 1 - 2 * half

    load_images = pltpu.make_async_copy(images, image_buf, load_sem.at[0])
    load_images.start()
    load_low = pltpu.make_async_copy(
        texts.at[pl.ds(0, half_rows)], text_all.at[t, 0], load_sem.at[1]
    )
    load_low.start()
    load_high = pltpu.make_async_copy(
        texts.at[pl.ds(half_rows, half_rows)], text_all.at[t, 1], load_sem.at[2]
    )
    load_high.start()
    load_audio = pltpu.make_async_copy(audio, window.at[0], load_sem.at[3])
    load_audio.start()

    barrier = pltpu.get_barrier_semaphore()

    def greet_plane(e):
        pl.semaphore_signal(
            barrier, inc=1, device_id=(t, lax.rem(a + e, n_aud)), device_id_type=MESH
        )

    def greet_line(d):
        pl.semaphore_signal(
            barrier, inc=1, device_id=(lax.rem(t + d, n_txt), a), device_id_type=MESH
        )

    each(n_aud, greet_plane, 1)
    each(n_txt, greet_line, 1)
    pl.semaphore_wait(barrier, n_aud + n_txt - 2)

    def audio_copy(k):
        return pltpu.make_async_remote_copy(
            src_ref=audio,
            dst_ref=window.at[k],
            send_sem=audio_send.at[k],
            recv_sem=audio_recv.at[k],
            device_id=(t, lax.rem(a + n_aud - k, n_aud)),
            device_id_type=MESH,
        )

    def gather_copy(d):
        return pltpu.make_async_remote_copy(
            src_ref=texts.at[pl.ds(pl.multiple_of(half * half_rows, half_rows), half_rows)],
            dst_ref=text_all.at[t, half],
            send_sem=gather_send.at[d],
            recv_sem=gather_recv.at[d],
            device_id=(lax.rem(t + d, n_txt), a),
            device_id_type=MESH,
        )

    def relay_copy(d):
        source = lax.rem(t + n_txt - d, n_txt)
        return pltpu.make_async_remote_copy(
            src_ref=text_all.at[source, half],
            dst_ref=text_all.at[source, half],
            send_sem=relay_send.at[d],
            recv_sem=relay_recv.at[d],
            device_id=(t, partner),
            device_id_type=MESH,
        )

    for k in range(1, HOPS + 1):
        audio_copy(k).start()
    each(n_txt, lambda d: gather_copy(d).start(), 1)

    temper = scale[0]
    offset = bias[0]

    load_images.wait()
    image_half[...] = image_buf[...].astype(jnp.bfloat16)
    window_acc[...] = jnp.zeros_like(window_acc)
    load_low.wait()
    load_high.wait()
    load_audio.wait()
    for k in range(1, HOPS + 1):
        audio_copy(k).wait()

    tile = min(width, 256)

    def scatter_copy(s, e):
        peer = lax.rem(a + e, n_aud)
        return pltpu.make_async_remote_copy(
            src_ref=text_out.at[s, peer],
            dst_ref=text_in.at[e, s],
            send_sem=scatter_send,
            recv_sem=scatter_recv,
            device_id=(t, peer),
            device_id_type=MESH,
        )

    def process(d):
        s = lax.rem(t + n_txt - d, n_txt)
        base = d * cols if isinstance(d, int) else pl.multiple_of(d * cols, cols)
        held = text_all[s].reshape(text_rows, width)
        for w in range(slots):
            row = window[w // block, pl.ds(w % block, 1), :]
            products[pl.ds(base + w * text_rows, text_rows), :] = (held * row).astype(
                jnp.bfloat16
            )
        logits = (
            temper
            * lax.dot_general(
                products[pl.ds(base, cols), :],
                image_half[...],
                (((1,), (1,)), ((), ())),
                preferred_element_type=jnp.float32,
            )
            + offset
        )
        local = pos_text[...] - s * text_rows
        inside = (local >= 0) & (local < text_rows)
        target = jnp.where(inside, pos_audio[...] * text_rows + local, -1)
        index = lax.broadcasted_iota(jnp.int32, logits.shape, 0)
        positive = jnp.where(index == target, 1.0, 0.0)
        slope = ((jax.nn.sigmoid(logits) - positive) * temper).astype(jnp.bfloat16)
        slopes[pl.ds(base, cols), :] = slope
        for first in range(0, width, tile):
            grad = jnp.dot(
                slope, image_half[:, first : first + tile], preferred_element_type=jnp.float32
            )
            text_part = held[:, first : first + tile]
            total = jnp.zeros((text_rows, tile), jnp.float32)
            for w in range(slots):
                part = grad[w * text_rows : (w + 1) * text_rows]
                total = total + part * window[
                    w // block, pl.ds(w % block, 1), pl.ds(first, tile)
                ]
                weighted = part * text_part
                folded = weighted[0:8]
                for r in range(8, text_rows, 8):
                    folded = folded + weighted[r : r + 8]
                window_acc[w, :, pl.ds(first, tile)] += folded
            for c in range(first // chunk_cols, (first + tile) // chunk_cols):
                for r in range(text_rows // chunk_rows):
                    text_out[s, r * n_col + c] = total[
                        r * chunk_rows : (r + 1) * chunk_rows,
                        c * chunk_cols - first : (c + 1) * chunk_cols - first,
                    ]
        each(n_aud, lambda e: scatter_copy(s, e).start(), 1)

    process(0)

    def pass_on(d):
        gather_copy(d).wait()
        relay_copy(d).start()

    each(n_txt, pass_on, 1)

    def next_block(d, carry):
        relay_copy(d).wait()
        process(d)
        return carry

    lax.fori_loop(1, n_txt, next_block, 0)

    for w in range(slots):
        home_out[w // block, pl.ds(w % block, 1), :] = jnp.sum(
            window_acc[w], axis=0, keepdims=True
        )

    def home_copy(k):
        return pltpu.make_async_remote_copy(
            src_ref=home_out.at[k],
            dst_ref=home_in.at[k],
            send_sem=home_send.at[k],
            recv_sem=home_recv.at[k],
            device_id=(t, lax.rem(a + k, n_aud)),
            device_id_type=MESH,
        )

    for k in range(1, HOPS + 1):
        home_copy(k).start()

    stores = []
    for number, first in enumerate(range(0, width, tile)):
        result_buf[:, first : first + tile] = lax.dot_general(
            slopes[...],
            products[:, first : first + tile],
            (((0,), (0,)), ((), ())),
            preferred_element_type=jnp.float32,
        )
        store = pltpu.make_async_copy(
            result_buf.at[:, pl.ds(first, tile)],
            grad_images.at[:, pl.ds(first, tile)],
            store_sem.at[number],
        )
        store.start()
        stores.append(store)

    arrived = text_in.at[pl.ds(1, n_aud - 1)]
    gathered = pltpu.make_async_remote_copy(
        src_ref=arrived,
        dst_ref=arrived,
        send_sem=scatter_send,
        recv_sem=scatter_recv,
        device_id=(t, partner),
        device_id_type=MESH,
    )
    gathered.wait_recv()
    for s in range(n_txt):
        total = text_out[s, a]
        for e in range(1, n_aud):
            total = total + text_in[e, s]
        text_sum[s] = total

    def z_copy(d):
        to = lax.rem(t + d, n_txt)
        return pltpu.make_async_remote_copy(
            src_ref=text_sum.at[to],
            dst_ref=text_z.at[t],
            send_sem=z_send.at[d],
            recv_sem=z_recv.at[d],
            device_id=(to, a),
            device_id_type=MESH,
        )

    def za_copy(d):
        return pltpu.make_async_remote_copy(
            src_ref=audio_sum,
            dst_ref=audio_z.at[t],
            send_sem=za_send.at[d],
            recv_sem=za_recv.at[d],
            device_id=(lax.rem(t + d, n_txt), a),
            device_id_type=MESH,
        )

    each(n_txt, lambda d: z_copy(d).start(), 1)
    text_z[t] = text_sum[t]

    total = home_out[0]
    for k in range(1, HOPS + 1):
        home_copy(k).wait()
        total = total + home_in[k]
    audio_sum[...] = total
    audio_z[t] = total
    each(n_txt, lambda d: za_copy(d).start(), 1)

    each(n_txt, lambda d: z_copy(d).wait(), 1)
    total = text_z[0]
    for s in range(1, n_txt):
        total = total + text_z[s]
    piece[...] = total
    pieces[a] = total

    def spread_copy(e):
        return pltpu.make_async_remote_copy(
            src_ref=piece,
            dst_ref=pieces.at[a],
            send_sem=spread_send.at[e],
            recv_sem=spread_recv.at[e],
            device_id=(t, lax.rem(a + e, n_aud)),
            device_id_type=MESH,
        )

    each(n_aud, lambda e: spread_copy(e).start(), 1)

    each(n_txt, lambda d: za_copy(d).wait(), 1)
    total = audio_z[0]
    for s in range(1, n_txt):
        total = total + audio_z[s]
    grad_audio[...] = total

    each(n_aud, lambda e: spread_copy(e).wait(), 1)
    for c in range(n_col):
        for r in range(text_rows // chunk_rows):
            grad_texts[
                r * chunk_rows : (r + 1) * chunk_rows, c * chunk_cols : (c + 1) * chunk_cols
            ] = pieces[r * n_col + c]

    gathered.wait_send()
    for store in stores:
        store.wait()


def shards(n_txt, n_aud, images, texts, audio, pos_text, pos_audio, logit_scale, logit_bias):
    rows, width = images.shape
    text_rows = texts.shape[0]
    block = audio.shape[0]
    slots = (HOPS + 1) * block
    cols = slots * text_rows
    n_col = min(n_aud, width // LANES)
    n_row = n_aud // n_col
    chunk = (text_rows // n_row, width // n_col)
    f32, bf16 = jnp.float32, jnp.bfloat16
    vmem = pl.BlockSpec(memory_space=pltpu.VMEM)
    smem = pl.BlockSpec(memory_space=pltpu.SMEM)
    anywhere = pl.BlockSpec(memory_space=pl.ANY)
    dma = pltpu.SemaphoreType.DMA
    return pl.pallas_call(
        functools.partial(kernel, n_txt, n_aud),
        out_shape=(
            jax.ShapeDtypeStruct((rows, width), f32),
            jax.ShapeDtypeStruct((text_rows, width), f32),
            jax.ShapeDtypeStruct((block, width), f32),
        ),
        in_specs=[anywhere, anywhere, anywhere, vmem, vmem, smem, smem],
        out_specs=(anywhere, vmem, vmem),
        scratch_shapes=[
            pltpu.VMEM((rows, width), f32),
            pltpu.VMEM((rows, width), bf16),
            pltpu.VMEM((n_txt, 2, text_rows // 2, width), f32),
            pltpu.VMEM((HOPS + 1, block, width), f32),
            pltpu.VMEM((n_txt * cols, width), bf16),
            pltpu.VMEM((n_txt * cols, rows), bf16),
            pltpu.VMEM((slots, 8, width), f32),
            pltpu.VMEM((n_txt, n_aud) + chunk, f32),
            pltpu.VMEM((n_aud, n_txt) + chunk, f32),
            pltpu.VMEM((n_txt,) + chunk, f32),
            pltpu.VMEM((n_txt,) + chunk, f32),
            pltpu.VMEM(chunk, f32),
            pltpu.VMEM((n_aud,) + chunk, f32),
            pltpu.VMEM((HOPS + 1, block, width), f32),
            pltpu.VMEM((HOPS + 1, block, width), f32),
            pltpu.VMEM((block, width), f32),
            pltpu.VMEM((n_txt, block, width), f32),
            pltpu.VMEM((rows, width), f32),
            dma((4,)),
            dma((n_txt,)),
            dma((n_txt,)),
            dma((n_txt,)),
            dma((n_txt,)),
            dma((HOPS + 1,)),
            dma((HOPS + 1,)),
            dma,
            dma,
            dma((HOPS + 1,)),
            dma((HOPS + 1,)),
            dma((n_txt,)),
            dma((n_txt,)),
            dma((n_txt,)),
            dma((n_txt,)),
            dma((n_aud,)),
            dma((n_aud,)),
            dma((max(1, width // 256),)),
        ],
        compiler_params=pltpu.CompilerParams(
            collective_id=0, has_side_effects=True, vmem_limit_bytes=56 * 1024 * 1024
        ),
        name="trilinear",
    )(
        images,
        texts,
        audio,
        pos_text.reshape(1, rows),
        pos_audio.reshape(1, rows),
        logit_scale,
        logit_bias,
    )


def solution(mesh):
    placed = (
        P(("txt", "aud"), None),
        P("txt", None),
        P("aud", None),
        P(("txt", "aud")),
        P(("txt", "aud")),
        P(),
        P(),
    )
    return jax.shard_map(
        functools.partial(shards, mesh.shape["txt"], mesh.shape["aud"]),
        mesh=mesh,
        in_specs=placed,
        out_specs=(P(("txt", "aud"), None), P("txt", None), P("aud", None)),
        check_vma=False,
    )
```

```python
import functools
import jax
import jax.numpy as jnp
from jax import lax
from jax.experimental import pallas as pl
from jax.experimental.pallas import tpu as pltpu
from jax.sharding import PartitionSpec as P

HOPS = 2
MESH = pl.DeviceIdType.MESH
LANES = 128


def each(count, body, start=0):
    if count - start <= 8:
        for i in range(start, count):
            body(i)
    else:
        lax.fori_loop(start, count, lambda i, c: (body(i), c)[1], 0)


def each_far_first(count, place, body):
    above = count - 1 - place

    def step(i):
        body(jnp.where(i < above, above - i, i + 1))

    each(count - 1, step)


def kernel(
    n_txt,
    n_aud,
    images,
    texts,
    audio,
    pos_text_in,
    pos_audio_in,
    scale_in,
    bias_in,
    grad_images,
    grad_texts,
    grad_audio,
    pos_text,
    pos_audio,
    scale,
    bias,
    image_buf,
    image_half,
    text_all,
    window,
    products,
    slopes,
    window_acc,
    text_out,
    text_in,
    text_sum,
    text_z,
    piece,
    pieces,
    home_out,
    home_in,
    audio_sum,
    audio_z,
    load_sem,
    gather_send,
    gather_recv,
    relay_send,
    relay_recv,
    audio_send,
    audio_recv,
    scatter_send,
    scatter_recv,
    home_send,
    home_recv,
    z_send,
    z_recv,
    za_send,
    za_recv,
    spread_send,
    spread_recv,
):
    t = lax.axis_index("txt")
    a = lax.axis_index("aud")
    text_rows, width = texts.shape
    half_rows = text_rows // 2
    block = audio.shape[0]
    slots = (HOPS + 1) * block
    cols = slots * text_rows
    chunk_rows, chunk_cols = piece.shape
    n_col = width // chunk_cols
    half = lax.rem(a, 2)
    other = 1 - half
    partner = a + 1 - 2 * half

    barrier = pltpu.get_barrier_semaphore()

    def greet_plane(e):
        pl.semaphore_signal(
            barrier, inc=1, device_id=(t, lax.rem(a + e, n_aud)), device_id_type=MESH
        )

    def greet_line(d):
        pl.semaphore_signal(
            barrier, inc=1, device_id=(lax.rem(t + d, n_txt), a), device_id_type=MESH
        )

    each(n_txt, greet_line, 1)
    each(n_aud, greet_plane, 1)

    load_low = pltpu.make_async_copy(
        texts.at[pl.ds(0, half_rows)], text_all.at[t, 0], load_sem.at[1]
    )
    load_low.start()
    load_high = pltpu.make_async_copy(
        texts.at[pl.ds(half_rows, half_rows)], text_all.at[t, 1], load_sem.at[2]
    )
    load_high.start()
    load_audio = pltpu.make_async_copy(audio, window.at[0], load_sem.at[3])
    load_audio.start()
    load_images = pltpu.make_async_copy(images, image_buf, load_sem.at[0])
    load_images.start()
    small = [
        pltpu.make_async_copy(src, dst, load_sem.at[4 + i])
        for i, (src, dst) in enumerate(
            (
                (pos_text_in, pos_text),
                (pos_audio_in, pos_audio),
                (scale_in, scale),
                (bias_in, bias),
            )
        )
    ]
    for load in small:
        load.start()
    load_low.wait()
    load_high.wait()
    load_audio.wait()
    pl.semaphore_wait(barrier, n_aud + n_txt - 2)

    def audio_copy(k):
        return pltpu.make_async_remote_copy(
            src_ref=window.at[0],
            dst_ref=window.at[k],
            send_sem=audio_send.at[k],
            recv_sem=audio_recv.at[k],
            device_id=(t, lax.rem(a + n_aud - k, n_aud)),
            device_id_type=MESH,
        )

    def gather_copy(d):
        return pltpu.make_async_remote_copy(
            src_ref=text_all.at[t, half],
            dst_ref=text_all.at[t, half],
            send_sem=gather_send.at[d],
            recv_sem=gather_recv.at[d],
            device_id=(lax.rem(t + d, n_txt), a),
            device_id_type=MESH,
        )

    def relay_copy(d):
        source = lax.rem(t + n_txt - d, n_txt)
        return pltpu.make_async_remote_copy(
            src_ref=text_all.at[source, half],
            dst_ref=text_all.at[source, half],
            send_sem=relay_send.at[d],
            recv_sem=relay_recv.at[d],
            device_id=(t, partner),
            device_id_type=MESH,
        )

    for k in range(1, HOPS + 1):
        audio_copy(k).start()
    each_far_first(n_txt, t, lambda d: gather_copy(d).start())

    for load in small:
        load.wait()
    temper = scale[0]
    offset = bias[0]

    load_images.wait()
    image_half[...] = image_buf[...].astype(jnp.bfloat16)
    window_acc[...] = jnp.zeros_like(window_acc)
    for k in range(1, HOPS + 1):
        audio_copy(k).wait()

    tile = min(width, 256)

    def scatter_copy(s, e):
        peer = lax.rem(a + e, n_aud)
        return pltpu.make_async_remote_copy(
            src_ref=text_out.at[s, peer],
            dst_ref=text_in.at[e, s],
            send_sem=scatter_send,
            recv_sem=scatter_recv,
            device_id=(t, peer),
            device_id_type=MESH,
        )

    def process(d):
        s = lax.rem(t + n_txt - d, n_txt)
        base = d * cols if isinstance(d, int) else pl.multiple_of(d * cols, cols)
        held = text_all[s].reshape(text_rows, width)
        for w in range(slots):
            row = window[w // block, pl.ds(w % block, 1), :]
            products[pl.ds(base + w * text_rows, text_rows), :] = (held * row).astype(
                jnp.bfloat16
            )
        logits = (
            temper
            * lax.dot_general(
                products[pl.ds(base, cols), :],
                image_half[...],
                (((1,), (1,)), ((), ())),
                preferred_element_type=jnp.float32,
            )
            + offset
        )
        local = pos_text[...] - s * text_rows
        inside = (local >= 0) & (local < text_rows)
        target = jnp.where(inside, pos_audio[...] * text_rows + local, -1)
        index = lax.broadcasted_iota(jnp.int32, logits.shape, 0)
        positive = jnp.where(index == target, 1.0, 0.0)
        slope = ((jax.nn.sigmoid(logits) - positive) * temper).astype(jnp.bfloat16)
        slopes[pl.ds(base, cols), :] = slope
        for first in range(0, width, tile):
            grad = jnp.dot(
                slope, image_half[:, first : first + tile], preferred_element_type=jnp.float32
            )
            text_part = held[:, first : first + tile]
            total = jnp.zeros((text_rows, tile), jnp.float32)
            for w in range(slots):
                part = grad[w * text_rows : (w + 1) * text_rows]
                total = total + part * window[
                    w // block, pl.ds(w % block, 1), pl.ds(first, tile)
                ]
                weighted = part * text_part
                folded = weighted[0:8]
                for r in range(8, text_rows, 8):
                    folded = folded + weighted[r : r + 8]
                window_acc[w, :, pl.ds(first, tile)] += folded
            for c in range(first // chunk_cols, (first + tile) // chunk_cols):
                for r in range(text_rows // chunk_rows):
                    text_out[s, r * n_col + c] = total[
                        r * chunk_rows : (r + 1) * chunk_rows,
                        c * chunk_cols - first : (c + 1) * chunk_cols - first,
                    ]
        each(n_aud, lambda e: scatter_copy(s, e).start(), 1)

    process(0)

    def pass_on(d):
        gather_copy(d).wait()
        relay_copy(d).start()

    each(n_txt, pass_on, 1)

    def next_block(d, carry):
        relay_copy(d).wait()
        process(d)
        return carry

    lax.fori_loop(1, n_txt, next_block, 0)

    for w in range(slots):
        home_out[w // block, pl.ds(w % block, 1), :] = jnp.sum(
            window_acc[w], axis=0, keepdims=True
        )

    def home_copy(k):
        return pltpu.make_async_remote_copy(
            src_ref=home_out.at[k],
            dst_ref=home_in.at[k],
            send_sem=home_send.at[k],
            recv_sem=home_recv.at[k],
            device_id=(t, lax.rem(a + k, n_aud)),
            device_id_type=MESH,
        )

    for k in range(1, HOPS + 1):
        home_copy(k).start()

    for first in range(0, width, tile):
        grad_images[:, first : first + tile] = lax.dot_general(
            slopes[...],
            products[:, first : first + tile],
            (((0,), (0,)), ((), ())),
            preferred_element_type=jnp.float32,
        )

    arrived = text_in.at[pl.ds(1, n_aud - 1)]
    gathered = pltpu.make_async_remote_copy(
        src_ref=arrived,
        dst_ref=arrived,
        send_sem=scatter_send,
        recv_sem=scatter_recv,
        device_id=(t, partner),
        device_id_type=MESH,
    )
    gathered.wait_recv()
    for s in range(n_txt):
        total = text_out[s, a]
        for e in range(1, n_aud):
            total = total + text_in[e, s]
        text_sum[s] = total

    def z_copy(d):
        to = lax.rem(t + d, n_txt)
        return pltpu.make_async_remote_copy(
            src_ref=text_sum.at[to],
            dst_ref=text_z.at[t],
            send_sem=z_send.at[d],
            recv_sem=z_recv.at[d],
            device_id=(to, a),
            device_id_type=MESH,
        )

    def za_copy(d):
        return pltpu.make_async_remote_copy(
            src_ref=audio_sum,
            dst_ref=audio_z.at[t],
            send_sem=za_send.at[d],
            recv_sem=za_recv.at[d],
            device_id=(lax.rem(t + d, n_txt), a),
            device_id_type=MESH,
        )

    each_far_first(n_txt, t, lambda d: z_copy(d).start())
    text_z[t] = text_sum[t]

    total = home_out[0]
    for k in range(1, HOPS + 1):
        home_copy(k).wait()
        total = total + home_in[k]
    audio_sum[...] = total
    audio_z[t] = total
    each_far_first(n_txt, t, lambda d: za_copy(d).start())

    each(n_txt, lambda d: z_copy(d).wait(), 1)
    total = text_z[0]
    for s in range(1, n_txt):
        total = total + text_z[s]
    piece[...] = total
    pieces[a] = total

    def spread_copy(e):
        return pltpu.make_async_remote_copy(
            src_ref=piece,
            dst_ref=pieces.at[a],
            send_sem=spread_send.at[e],
            recv_sem=spread_recv.at[e],
            device_id=(t, lax.rem(a + e, n_aud)),
            device_id_type=MESH,
        )

    each(n_aud, lambda e: spread_copy(e).start(), 1)

    each(n_txt, lambda d: za_copy(d).wait(), 1)
    total = audio_z[0]
    for s in range(1, n_txt):
        total = total + audio_z[s]
    grad_audio[...] = total

    each(n_aud, lambda e: spread_copy(e).wait(), 1)
    for c in range(n_col):
        for r in range(text_rows // chunk_rows):
            grad_texts[
                r * chunk_rows : (r + 1) * chunk_rows, c * chunk_cols : (c + 1) * chunk_cols
            ] = pieces[r * n_col + c]

    gathered.wait_send()


def put_out(*refs):
    count = len(refs) // 2
    sems = refs[-1]
    copies = [
        pltpu.make_async_copy(refs[i], refs[count + i], sems.at[i]) for i in range(count)
    ]
    for copy in copies:
        copy.start()
    for copy in copies:
        copy.wait()


def shards(n_txt, n_aud, images, texts, audio, pos_text, pos_audio, logit_scale, logit_bias):
    rows, width = images.shape
    text_rows = texts.shape[0]
    block = audio.shape[0]
    slots = (HOPS + 1) * block
    cols = slots * text_rows
    n_col = min(n_aud, width // LANES)
    n_row = n_aud // n_col
    chunk = (text_rows // n_row, width // n_col)
    f32, bf16 = jnp.float32, jnp.bfloat16
    vmem = pl.BlockSpec(memory_space=pltpu.VMEM)
    anywhere = pl.BlockSpec(memory_space=pltpu.HBM)
    dma = pltpu.SemaphoreType.DMA
    shapes = ((rows, width), (text_rows, width), (block, width))
    held = pl.pallas_call(
        functools.partial(kernel, n_txt, n_aud),
        out_shape=tuple(pltpu.VMEM(shape, f32) for shape in shapes),
        in_specs=[anywhere] * 7,
        out_specs=(vmem,) * 3,
        scratch_shapes=[
            pltpu.VMEM((1, rows), jnp.int32),
            pltpu.VMEM((1, rows), jnp.int32),
            pltpu.SMEM((1,), f32),
            pltpu.SMEM((1,), f32),
            pltpu.VMEM((rows, width), f32),
            pltpu.VMEM((rows, width), bf16),
            pltpu.VMEM((n_txt, 2, text_rows // 2, width), f32),
            pltpu.VMEM((HOPS + 1, block, width), f32),
            pltpu.VMEM((n_txt * cols, width), bf16),
            pltpu.VMEM((n_txt * cols, rows), bf16),
            pltpu.VMEM((slots, 8, width), f32),
            pltpu.VMEM((n_txt, n_aud) + chunk, f32),
            pltpu.VMEM((n_aud, n_txt) + chunk, f32),
            pltpu.VMEM((n_txt,) + chunk, f32),
            pltpu.VMEM((n_txt,) + chunk, f32),
            pltpu.VMEM(chunk, f32),
            pltpu.VMEM((n_aud,) + chunk, f32),
            pltpu.VMEM((HOPS + 1, block, width), f32),
            pltpu.VMEM((HOPS + 1, block, width), f32),
            pltpu.VMEM((block, width), f32),
            pltpu.VMEM((n_txt, block, width), f32),
            dma((8,)),
            dma((n_txt,)),
            dma((n_txt,)),
            dma((n_txt,)),
            dma((n_txt,)),
            dma((HOPS + 1,)),
            dma((HOPS + 1,)),
            dma,
            dma,
            dma((HOPS + 1,)),
            dma((HOPS + 1,)),
            dma((n_txt,)),
            dma((n_txt,)),
            dma((n_txt,)),
            dma((n_txt,)),
            dma((n_aud,)),
            dma((n_aud,)),
        ],
        compiler_params=pltpu.CompilerParams(
            collective_id=0, has_side_effects=True, vmem_limit_bytes=56 * 1024 * 1024
        ),
        name="trilinear",
    )(
        images,
        texts,
        audio,
        pos_text.reshape(1, rows),
        pos_audio.reshape(1, rows),
        logit_scale,
        logit_bias,
    )
    return pl.pallas_call(
        put_out,
        out_shape=tuple(jax.ShapeDtypeStruct(shape, f32) for shape in shapes),
        in_specs=[vmem] * 3,
        out_specs=(anywhere,) * 3,
        scratch_shapes=[dma((3,))],
        name="put_out",
    )(*[pltpu.with_memory_space_constraint(h, pltpu.VMEM) for h in held])


def solution(mesh):
    placed = (
        P(("txt", "aud"), None),
        P("txt", None),
        P("aud", None),
        P(("txt", "aud")),
        P(("txt", "aud")),
        P(),
        P(),
    )
    return jax.shard_map(
        functools.partial(shards, mesh.shape["txt"], mesh.shape["aud"]),
        mesh=mesh,
        in_specs=placed,
        out_specs=(P(("txt", "aud"), None), P("txt", None), P("aud", None)),
        check_vma=False,
    )
```

```python
import functools
import jax
import jax.numpy as jnp
from jax import lax
from jax.experimental import pallas as pl
from jax.experimental.pallas import tpu as pltpu
from jax.sharding import PartitionSpec as P

HOPS = 2
MESH = pl.DeviceIdType.MESH
LANES = 128


def each(count, body, start=0):
    if count - start <= 8:
        for i in range(start, count):
            body(i)
    else:
        lax.fori_loop(start, count, lambda i, c: (body(i), c)[1], 0)


def each_far_first(count, place, body):
    above = count - 1 - place

    def step(i):
        body(jnp.where(i < above, above - i, i + 1))

    each(count - 1, step)


def kernel(
    n_txt,
    n_aud,
    images,
    texts,
    audio,
    pos_text_in,
    pos_audio_in,
    scale_in,
    bias_in,
    grad_images,
    grad_texts,
    grad_audio,
    pos_text,
    pos_audio,
    scale,
    bias,
    image_buf,
    image_half,
    text_all,
    window,
    products,
    slopes,
    window_acc,
    text_out,
    text_in,
    text_sum,
    text_z,
    piece,
    pieces,
    home_out,
    home_in,
    audio_sum,
    audio_z,
    load_sem,
    gather_send,
    gather_recv,
    relay_send,
    relay_recv,
    audio_send,
    audio_recv,
    scatter_send,
    scatter_recv,
    home_send,
    home_recv,
    z_send,
    z_recv,
    za_send,
    za_recv,
    spread_send,
    spread_recv,
):
    t = lax.axis_index("txt")
    a = lax.axis_index("aud")
    text_rows, width = texts.shape
    half_rows = text_rows // 2
    block = audio.shape[0]
    slots = (HOPS + 1) * block
    cols = slots * text_rows
    chunk_rows, chunk_cols = piece.shape
    n_col = width // chunk_cols
    half = lax.rem(a, 2)
    partner = a + 1 - 2 * half

    barrier = pltpu.get_barrier_semaphore()

    def greet_plane(e):
        pl.semaphore_signal(
            barrier, inc=1, device_id=(t, lax.rem(a + e, n_aud)), device_id_type=MESH
        )

    def greet_line(d):
        pl.semaphore_signal(
            barrier, inc=1, device_id=(lax.rem(t + d, n_txt), a), device_id_type=MESH
        )

    each(n_txt, greet_line, 1)
    each(n_aud, greet_plane, 1)

    load_low = pltpu.make_async_copy(
        texts.at[pl.ds(0, half_rows)], text_all.at[t, 0], load_sem.at[1]
    )
    load_low.start()
    load_high = pltpu.make_async_copy(
        texts.at[pl.ds(half_rows, half_rows)], text_all.at[t, 1], load_sem.at[2]
    )
    load_high.start()
    load_audio = pltpu.make_async_copy(audio, window.at[0], load_sem.at[3])
    load_audio.start()
    load_images = pltpu.make_async_copy(images, image_buf, load_sem.at[0])
    load_images.start()
    small = [
        pltpu.make_async_copy(src, dst, load_sem.at[4 + i])
        for i, (src, dst) in enumerate(
            (
                (pos_text_in, pos_text),
                (pos_audio_in, pos_audio),
                (scale_in, scale),
                (bias_in, bias),
            )
        )
    ]
    for load in small:
        load.start()
    load_low.wait()
    load_high.wait()
    load_audio.wait()
    pl.semaphore_wait(barrier, n_aud + n_txt - 2)

    def audio_copy(k):
        return pltpu.make_async_remote_copy(
            src_ref=window.at[0],
            dst_ref=window.at[k],
            send_sem=audio_send.at[k],
            recv_sem=audio_recv.at[k],
            device_id=(t, lax.rem(a + n_aud - k, n_aud)),
            device_id_type=MESH,
        )

    def gather_copy(d):
        return pltpu.make_async_remote_copy(
            src_ref=text_all.at[t, half],
            dst_ref=text_all.at[t, half],
            send_sem=gather_send.at[d],
            recv_sem=gather_recv.at[d],
            device_id=(lax.rem(t + d, n_txt), a),
            device_id_type=MESH,
        )

    def relay_copy(d):
        source = lax.rem(t + n_txt - d, n_txt)
        return pltpu.make_async_remote_copy(
            src_ref=text_all.at[source, half],
            dst_ref=text_all.at[source, half],
            send_sem=relay_send.at[d],
            recv_sem=relay_recv.at[d],
            device_id=(t, partner),
            device_id_type=MESH,
        )

    for k in range(1, HOPS + 1):
        audio_copy(k).start()
    each_far_first(n_txt, t, lambda d: gather_copy(d).start())

    for load in small:
        load.wait()
    temper = scale[0]
    offset = bias[0]

    load_images.wait()
    image_half[...] = image_buf[...].astype(jnp.bfloat16)
    window_acc[...] = jnp.zeros_like(window_acc)
    for k in range(1, HOPS + 1):
        audio_copy(k).wait()

    tile = min(width, 256)

    def scatter_copy(turn, s, e):
        peer = lax.rem(a + e, n_aud)
        return pltpu.make_async_remote_copy(
            src_ref=text_out.at[s, peer],
            dst_ref=text_in.at[s, e],
            send_sem=scatter_send,
            recv_sem=scatter_recv.at[turn],
            device_id=(t, peer),
            device_id_type=MESH,
        )

    def owner(turn):
        low_first = jnp.where(turn <= t, t + 1 - turn, turn)
        high_first = jnp.where(turn < n_txt - t, t + turn, n_txt - turn)
        return jnp.where(2 * t >= n_txt, low_first, high_first)

    def process(turn, d):
        s = lax.rem(t + n_txt - d, n_txt)
        base = turn * cols if isinstance(turn, int) else pl.multiple_of(turn * cols, cols)
        held = text_all[s].reshape(text_rows, width)
        for w in range(slots):
            row = window[w // block, pl.ds(w % block, 1), :]
            products[pl.ds(base + w * text_rows, text_rows), :] = (held * row).astype(
                jnp.bfloat16
            )
        logits = (
            temper
            * lax.dot_general(
                products[pl.ds(base, cols), :],
                image_half[...],
                (((1,), (1,)), ((), ())),
                preferred_element_type=jnp.float32,
            )
            + offset
        )
        local = pos_text[...] - s * text_rows
        inside = (local >= 0) & (local < text_rows)
        target = jnp.where(inside, pos_audio[...] * text_rows + local, -1)
        index = lax.broadcasted_iota(jnp.int32, logits.shape, 0)
        positive = jnp.where(index == target, 1.0, 0.0)
        slope = ((jax.nn.sigmoid(logits) - positive) * temper).astype(jnp.bfloat16)
        slopes[pl.ds(base, cols), :] = slope
        for first in range(0, width, tile):
            grad = jnp.dot(
                slope, image_half[:, first : first + tile], preferred_element_type=jnp.float32
            )
            text_part = held[:, first : first + tile]
            total = jnp.zeros((text_rows, tile), jnp.float32)
            for w in range(slots):
                part = grad[w * text_rows : (w + 1) * text_rows]
                total = total + part * window[
                    w // block, pl.ds(w % block, 1), pl.ds(first, tile)
                ]
                weighted = part * text_part
                folded = weighted[0:8]
                for r in range(8, text_rows, 8):
                    folded = folded + weighted[r : r + 8]
                window_acc[w, :, pl.ds(first, tile)] += folded
            for c in range(first // chunk_cols, (first + tile) // chunk_cols):
                for r in range(text_rows // chunk_rows):
                    text_out[s, r * n_col + c] = total[
                        r * chunk_rows : (r + 1) * chunk_rows,
                        c * chunk_cols - first : (c + 1) * chunk_cols - first,
                    ]
        each(n_aud, lambda e: scatter_copy(turn, s, e).start(), 1)

    process(0, 0)

    def pass_on(turn):
        d = owner(turn)
        gather_copy(d).wait()
        relay_copy(d).start()

    each(n_txt, pass_on, 1)

    def next_block(turn, carry):
        d = owner(turn)
        relay_copy(d).wait()
        process(turn, d)
        return carry

    lax.fori_loop(1, n_txt, next_block, 0)

    for w in range(slots):
        home_out[w // block, pl.ds(w % block, 1), :] = jnp.sum(
            window_acc[w], axis=0, keepdims=True
        )

    def home_copy(k):
        return pltpu.make_async_remote_copy(
            src_ref=home_out.at[k],
            dst_ref=home_in.at[k],
            send_sem=home_send.at[k],
            recv_sem=home_recv.at[k],
            device_id=(t, lax.rem(a + k, n_aud)),
            device_id_type=MESH,
        )

    for k in range(1, HOPS + 1):
        home_copy(k).start()

    for first in range(0, width, tile):
        grad_images[:, first : first + tile] = lax.dot_general(
            slopes[...],
            products[:, first : first + tile],
            (((0,), (0,)), ((), ())),
            preferred_element_type=jnp.float32,
        )

    def reduced(turn, s):
        arrived = text_in.at[s, pl.ds(1, n_aud - 1)]
        pltpu.make_async_remote_copy(
            src_ref=arrived,
            dst_ref=arrived,
            send_sem=scatter_send,
            recv_sem=scatter_recv.at[turn],
            device_id=(t, partner),
            device_id_type=MESH,
        ).wait_recv()
        total = text_out[s, a]
        for e in range(1, n_aud):
            total = total + text_in[s, e]
        return total

    def z_copy(d):
        to = lax.rem(t + d, n_txt)
        return pltpu.make_async_remote_copy(
            src_ref=text_sum.at[to],
            dst_ref=text_z.at[t],
            send_sem=z_send.at[d],
            recv_sem=z_recv.at[d],
            device_id=(to, a),
            device_id_type=MESH,
        )

    def za_copy(d):
        return pltpu.make_async_remote_copy(
            src_ref=audio_sum,
            dst_ref=audio_z.at[t],
            send_sem=za_send.at[d],
            recv_sem=za_recv.at[d],
            device_id=(lax.rem(t + d, n_txt), a),
            device_id_type=MESH,
        )

    def send_back(turn):
        d = owner(turn)
        s = lax.rem(t + n_txt - d, n_txt)
        text_sum[s] = reduced(turn, s)
        z_copy(n_txt - d).start()

    each(n_txt - 1, send_back, 1)

    total = home_out[0]
    for k in range(1, HOPS + 1):
        home_copy(k).wait()
        total = total + home_in[k]
    audio_sum[...] = total
    audio_z[t] = total
    each_far_first(n_txt, t, lambda d: za_copy(d).start())

    send_back(n_txt - 1)
    text_z[t] = reduced(0, t)
    each(n_txt, lambda d: z_copy(d).wait(), 1)
    total = text_z[0]
    for s in range(1, n_txt):
        total = total + text_z[s]
    piece[...] = total
    pieces[a] = total

    def spread_copy(e):
        return pltpu.make_async_remote_copy(
            src_ref=piece,
            dst_ref=pieces.at[a],
            send_sem=spread_send.at[e],
            recv_sem=spread_recv.at[e],
            device_id=(t, lax.rem(a + e, n_aud)),
            device_id_type=MESH,
        )

    each(n_aud, lambda e: spread_copy(e).start(), 1)

    each(n_txt, lambda d: za_copy(d).wait(), 1)
    total = audio_z[0]
    for s in range(1, n_txt):
        total = total + audio_z[s]
    grad_audio[...] = total

    each(n_aud, lambda e: spread_copy(e).wait(), 1)
    for c in range(n_col):
        for r in range(text_rows // chunk_rows):
            grad_texts[
                r * chunk_rows : (r + 1) * chunk_rows, c * chunk_cols : (c + 1) * chunk_cols
            ] = pieces[r * n_col + c]

    sent = text_in.at[:, pl.ds(1, n_aud - 1)]
    pltpu.make_async_remote_copy(
        src_ref=sent,
        dst_ref=sent,
        send_sem=scatter_send,
        recv_sem=scatter_recv.at[0],
        device_id=(t, partner),
        device_id_type=MESH,
    ).wait_send()


def put_out(*refs):
    count = len(refs) // 2
    sems = refs[-1]
    copies = [
        pltpu.make_async_copy(refs[i], refs[count + i], sems.at[i]) for i in range(count)
    ]
    for copy in copies:
        copy.start()
    for copy in copies:
        copy.wait()


def shards(n_txt, n_aud, images, texts, audio, pos_text, pos_audio, logit_scale, logit_bias):
    rows, width = images.shape
    text_rows = texts.shape[0]
    block = audio.shape[0]
    slots = (HOPS + 1) * block
    cols = slots * text_rows
    n_col = min(n_aud, width // LANES)
    n_row = n_aud // n_col
    chunk = (text_rows // n_row, width // n_col)
    f32, bf16 = jnp.float32, jnp.bfloat16
    vmem = pl.BlockSpec(memory_space=pltpu.VMEM)
    anywhere = pl.BlockSpec(memory_space=pltpu.HBM)
    dma = pltpu.SemaphoreType.DMA
    shapes = ((rows, width), (text_rows, width), (block, width))
    held = pl.pallas_call(
        functools.partial(kernel, n_txt, n_aud),
        out_shape=tuple(pltpu.VMEM(shape, f32) for shape in shapes),
        in_specs=[anywhere] * 7,
        out_specs=(vmem,) * 3,
        scratch_shapes=[
            pltpu.VMEM((1, rows), jnp.int32),
            pltpu.VMEM((1, rows), jnp.int32),
            pltpu.SMEM((1,), f32),
            pltpu.SMEM((1,), f32),
            pltpu.VMEM((rows, width), f32),
            pltpu.VMEM((rows, width), bf16),
            pltpu.VMEM((n_txt, 2, text_rows // 2, width), f32),
            pltpu.VMEM((HOPS + 1, block, width), f32),
            pltpu.VMEM((n_txt * cols, width), bf16),
            pltpu.VMEM((n_txt * cols, rows), bf16),
            pltpu.VMEM((slots, 8, width), f32),
            pltpu.VMEM((n_txt, n_aud) + chunk, f32),
            pltpu.VMEM((n_txt, n_aud) + chunk, f32),
            pltpu.VMEM((n_txt,) + chunk, f32),
            pltpu.VMEM((n_txt,) + chunk, f32),
            pltpu.VMEM(chunk, f32),
            pltpu.VMEM((n_aud,) + chunk, f32),
            pltpu.VMEM((HOPS + 1, block, width), f32),
            pltpu.VMEM((HOPS + 1, block, width), f32),
            pltpu.VMEM((block, width), f32),
            pltpu.VMEM((n_txt, block, width), f32),
            dma((8,)),
            dma((n_txt,)),
            dma((n_txt,)),
            dma((n_txt,)),
            dma((n_txt,)),
            dma((HOPS + 1,)),
            dma((HOPS + 1,)),
            dma,
            dma((n_txt,)),
            dma((HOPS + 1,)),
            dma((HOPS + 1,)),
            dma((n_txt,)),
            dma((n_txt,)),
            dma((n_txt,)),
            dma((n_txt,)),
            dma((n_aud,)),
            dma((n_aud,)),
        ],
        compiler_params=pltpu.CompilerParams(
            collective_id=0, has_side_effects=True, vmem_limit_bytes=56 * 1024 * 1024
        ),
        name="trilinear",
    )(
        images,
        texts,
        audio,
        pos_text.reshape(1, rows),
        pos_audio.reshape(1, rows),
        logit_scale,
        logit_bias,
    )
    return pl.pallas_call(
        put_out,
        out_shape=tuple(jax.ShapeDtypeStruct(shape, f32) for shape in shapes),
        in_specs=[vmem] * 3,
        out_specs=(anywhere,) * 3,
        scratch_shapes=[dma((3,))],
        name="put_out",
    )(*[pltpu.with_memory_space_constraint(h, pltpu.VMEM) for h in held])


def solution(mesh):
    placed = (
        P(("txt", "aud"), None),
        P("txt", None),
        P("aud", None),
        P(("txt", "aud")),
        P(("txt", "aud")),
        P(),
        P(),
    )
    return jax.shard_map(
        functools.partial(shards, mesh.shape["txt"], mesh.shape["aud"]),
        mesh=mesh,
        in_specs=placed,
        out_specs=(P(("txt", "aud"), None), P("txt", None), P("aud", None)),
        check_vma=False,
    )
```

```python
import functools
import jax
import jax.numpy as jnp
from jax import lax
from jax.experimental import pallas as pl
from jax.experimental.pallas import tpu as pltpu
from jax.sharding import PartitionSpec as P

HOPS = 2
MESH = pl.DeviceIdType.MESH
LANES = 128


def each(count, body, start=0):
    if count - start <= 8:
        for i in range(start, count):
            body(i)
    else:
        lax.fori_loop(start, count, lambda i, c: (body(i), c)[1], 0)


def each_far_first(count, place, body):
    above = count - 1 - place

    def step(i):
        body(jnp.where(i < above, above - i, i + 1))

    each(count - 1, step)


def kernel(
    n_txt,
    n_aud,
    images,
    texts,
    audio,
    pos_text_in,
    pos_audio_in,
    scale_in,
    bias_in,
    grad_images,
    grad_texts,
    grad_audio,
    pos_text,
    pos_audio,
    scale,
    bias,
    image_buf,
    image_half,
    text_all,
    window,
    products,
    slopes,
    window_acc,
    text_out,
    text_in,
    text_sum,
    text_z,
    piece,
    pieces,
    home_out,
    home_in,
    audio_sum,
    audio_z,
    load_sem,
    gather_send,
    gather_recv,
    relay_send,
    relay_recv,
    audio_send,
    audio_recv,
    scatter_send,
    scatter_recv,
    home_send,
    home_recv,
    z_send,
    z_recv,
    za_send,
    za_recv,
    spread_send,
    spread_recv,
):
    t = lax.axis_index("txt")
    a = lax.axis_index("aud")
    text_rows, width = texts.shape
    half_rows = text_rows // 2
    block = audio.shape[0]
    slots = (HOPS + 1) * block
    cols = slots * text_rows
    chunk_rows, chunk_cols = piece.shape
    n_col = width // chunk_cols
    half = lax.rem(a, 2)
    partner = a + 1 - 2 * half

    barrier = pltpu.get_barrier_semaphore()

    def greet_plane(e):
        pl.semaphore_signal(
            barrier, inc=1, device_id=(t, lax.rem(a + e, n_aud)), device_id_type=MESH
        )

    def greet_line(d):
        pl.semaphore_signal(
            barrier, inc=1, device_id=(lax.rem(t + d, n_txt), a), device_id_type=MESH
        )

    each(n_txt, greet_line, 1)
    each(n_aud, greet_plane, 1)

    load_low = pltpu.make_async_copy(
        texts.at[pl.ds(0, half_rows)], text_all.at[t, 0], load_sem.at[1]
    )
    load_low.start()
    load_high = pltpu.make_async_copy(
        texts.at[pl.ds(half_rows, half_rows)], text_all.at[t, 1], load_sem.at[2]
    )
    load_high.start()
    load_audio = pltpu.make_async_copy(audio, window.at[0], load_sem.at[3])
    load_audio.start()
    load_images = pltpu.make_async_copy(images, image_buf, load_sem.at[0])
    load_images.start()
    small = [
        pltpu.make_async_copy(src, dst, load_sem.at[4 + i])
        for i, (src, dst) in enumerate(
            (
                (pos_text_in, pos_text),
                (pos_audio_in, pos_audio),
                (scale_in, scale),
                (bias_in, bias),
            )
        )
    ]
    for load in small:
        load.start()
    load_low.wait()
    load_high.wait()
    load_audio.wait()
    pl.semaphore_wait(barrier, n_aud + n_txt - 2)

    def audio_copy(k):
        return pltpu.make_async_remote_copy(
            src_ref=window.at[0],
            dst_ref=window.at[k],
            send_sem=audio_send.at[k],
            recv_sem=audio_recv.at[k],
            device_id=(t, lax.rem(a + n_aud - k, n_aud)),
            device_id_type=MESH,
        )

    def gather_copy(d):
        return pltpu.make_async_remote_copy(
            src_ref=text_all.at[t, half],
            dst_ref=text_all.at[t, half],
            send_sem=gather_send.at[d],
            recv_sem=gather_recv.at[d],
            device_id=(lax.rem(t + d, n_txt), a),
            device_id_type=MESH,
        )

    def relay_copy(d):
        source = lax.rem(t + n_txt - d, n_txt)
        return pltpu.make_async_remote_copy(
            src_ref=text_all.at[source, half],
            dst_ref=text_all.at[source, half],
            send_sem=relay_send.at[d],
            recv_sem=relay_recv.at[d],
            device_id=(t, partner),
            device_id_type=MESH,
        )

    for k in range(1, HOPS + 1):
        audio_copy(k).start()
    each_far_first(n_txt, t, lambda d: gather_copy(d).start())

    for load in small:
        load.wait()
    temper = scale[0]
    offset = bias[0]

    load_images.wait()
    image_half[...] = image_buf[...].astype(jnp.bfloat16)
    window_acc[...] = jnp.zeros_like(window_acc)
    for k in range(1, HOPS + 1):
        audio_copy(k).wait()

    tile = min(width, 256)

    def scatter_copy(turn, s, e):
        peer = lax.rem(a + e, n_aud)
        return pltpu.make_async_remote_copy(
            src_ref=text_out.at[s, peer],
            dst_ref=text_in.at[s, e],
            send_sem=scatter_send,
            recv_sem=scatter_recv.at[turn],
            device_id=(t, peer),
            device_id_type=MESH,
        )

    def owner(turn):
        low_first = jnp.where(turn <= t, t + 1 - turn, turn)
        high_first = jnp.where(turn < n_txt - t, t + turn, n_txt - turn)
        return jnp.where(2 * t >= n_txt, low_first, high_first)

    def process(turn, d):
        s = lax.rem(t + n_txt - d, n_txt)
        base = turn * cols if isinstance(turn, int) else pl.multiple_of(turn * cols, cols)
        held = text_all[s].reshape(text_rows, width)
        for w in range(slots):
            row = window[w // block, pl.ds(w % block, 1), :]
            products[pl.ds(base + w * text_rows, text_rows), :] = (held * row).astype(
                jnp.bfloat16
            )
        logits = (
            temper
            * lax.dot_general(
                products[pl.ds(base, cols), :],
                image_half[...],
                (((1,), (1,)), ((), ())),
                preferred_element_type=jnp.float32,
            )
            + offset
        )
        local = pos_text[...] - s * text_rows
        inside = (local >= 0) & (local < text_rows)
        target = jnp.where(inside, pos_audio[...] * text_rows + local, -1)
        index = lax.broadcasted_iota(jnp.int32, logits.shape, 0)
        positive = jnp.where(index == target, 1.0, 0.0)
        slope = ((jax.nn.sigmoid(logits) - positive) * temper).astype(jnp.bfloat16)
        slopes[pl.ds(base, cols), :] = slope
        for first in range(0, width, tile):
            grad = jnp.dot(
                slope, image_half[:, first : first + tile], preferred_element_type=jnp.float32
            )
            text_part = held[:, first : first + tile]
            total = jnp.zeros((text_rows, tile), jnp.float32)
            for w in range(slots):
                part = grad[w * text_rows : (w + 1) * text_rows]
                total = total + part * window[
                    w // block, pl.ds(w % block, 1), pl.ds(first, tile)
                ]
                weighted = part * text_part
                folded = weighted[0:8]
                for r in range(8, text_rows, 8):
                    folded = folded + weighted[r : r + 8]
                window_acc[w, :, pl.ds(first, tile)] += folded
            for c in range(first // chunk_cols, (first + tile) // chunk_cols):
                for r in range(text_rows // chunk_rows):
                    text_out[s, r * n_col + c] = total[
                        r * chunk_rows : (r + 1) * chunk_rows,
                        c * chunk_cols - first : (c + 1) * chunk_cols - first,
                    ]
        each(n_aud, lambda e: scatter_copy(turn, s, e).start(), 1)

    def pass_on(turn):
        d = owner(turn)
        gather_copy(d).wait()
        relay_copy(d).start()

    each(n_txt, pass_on, 1)
    process(0, 0)

    def next_block(turn, carry):
        d = owner(turn)
        relay_copy(d).wait()
        process(turn, d)
        return carry

    lax.fori_loop(1, n_txt, next_block, 0)

    for w in range(slots):
        home_out[w // block, pl.ds(w % block, 1), :] = jnp.sum(
            window_acc[w], axis=0, keepdims=True
        )

    def home_copy(k):
        return pltpu.make_async_remote_copy(
            src_ref=home_out.at[k],
            dst_ref=home_in.at[k],
            send_sem=home_send.at[k],
            recv_sem=home_recv.at[k],
            device_id=(t, lax.rem(a + k, n_aud)),
            device_id_type=MESH,
        )

    for k in range(1, HOPS + 1):
        home_copy(k).start()

    for first in range(0, width, tile):
        grad_images[:, first : first + tile] = lax.dot_general(
            slopes[...],
            products[:, first : first + tile],
            (((0,), (0,)), ((), ())),
            preferred_element_type=jnp.float32,
        )

    def reduced(turn, s):
        arrived = text_in.at[s, pl.ds(1, n_aud - 1)]
        pltpu.make_async_remote_copy(
            src_ref=arrived,
            dst_ref=arrived,
            send_sem=scatter_send,
            recv_sem=scatter_recv.at[turn],
            device_id=(t, partner),
            device_id_type=MESH,
        ).wait_recv()
        total = text_out[s, a]
        for e in range(1, n_aud):
            total = total + text_in[s, e]
        return total

    def z_copy(d):
        to = lax.rem(t + d, n_txt)
        return pltpu.make_async_remote_copy(
            src_ref=text_sum.at[to],
            dst_ref=text_z.at[t],
            send_sem=z_send.at[d],
            recv_sem=z_recv.at[d],
            device_id=(to, a),
            device_id_type=MESH,
        )

    def za_copy(d):
        return pltpu.make_async_remote_copy(
            src_ref=audio_sum,
            dst_ref=audio_z.at[t],
            send_sem=za_send.at[d],
            recv_sem=za_recv.at[d],
            device_id=(lax.rem(t + d, n_txt), a),
            device_id_type=MESH,
        )

    def send_back(turn):
        d = owner(turn)
        s = lax.rem(t + n_txt - d, n_txt)
        text_sum[s] = reduced(turn, s)
        z_copy(n_txt - d).start()

    each(n_txt - 1, send_back, 1)

    total = home_out[0]
    for k in range(1, HOPS + 1):
        home_copy(k).wait()
        total = total + home_in[k]
    audio_sum[...] = total
    audio_z[t] = total
    each_far_first(n_txt, t, lambda d: za_copy(d).start())

    send_back(n_txt - 1)
    text_z[t] = reduced(0, t)
    each(n_txt, lambda d: z_copy(d).wait(), 1)
    total = text_z[0]
    for s in range(1, n_txt):
        total = total + text_z[s]
    piece[...] = total
    pieces[a] = total

    def spread_copy(e):
        return pltpu.make_async_remote_copy(
            src_ref=piece,
            dst_ref=pieces.at[a],
            send_sem=spread_send.at[e],
            recv_sem=spread_recv.at[e],
            device_id=(t, lax.rem(a + e, n_aud)),
            device_id_type=MESH,
        )

    each(n_aud, lambda e: spread_copy(e).start(), 1)

    each(n_txt, lambda d: za_copy(d).wait(), 1)
    total = audio_z[0]
    for s in range(1, n_txt):
        total = total + audio_z[s]
    grad_audio[...] = total

    each(n_aud, lambda e: spread_copy(e).wait(), 1)
    for c in range(n_col):
        for r in range(text_rows // chunk_rows):
            grad_texts[
                r * chunk_rows : (r + 1) * chunk_rows, c * chunk_cols : (c + 1) * chunk_cols
            ] = pieces[r * n_col + c]

    sent = text_in.at[:, pl.ds(1, n_aud - 1)]
    pltpu.make_async_remote_copy(
        src_ref=sent,
        dst_ref=sent,
        send_sem=scatter_send,
        recv_sem=scatter_recv.at[0],
        device_id=(t, partner),
        device_id_type=MESH,
    ).wait_send()


def put_out(*refs):
    count = len(refs) // 2
    sems = refs[-1]
    copies = [
        pltpu.make_async_copy(refs[i], refs[count + i], sems.at[i]) for i in range(count)
    ]
    for copy in copies:
        copy.start()
    for copy in copies:
        copy.wait()


def shards(n_txt, n_aud, images, texts, audio, pos_text, pos_audio, logit_scale, logit_bias):
    rows, width = images.shape
    text_rows = texts.shape[0]
    block = audio.shape[0]
    slots = (HOPS + 1) * block
    cols = slots * text_rows
    n_col = min(n_aud, width // LANES)
    n_row = n_aud // n_col
    chunk = (text_rows // n_row, width // n_col)
    f32, bf16 = jnp.float32, jnp.bfloat16
    vmem = pl.BlockSpec(memory_space=pltpu.VMEM)
    anywhere = pl.BlockSpec(memory_space=pltpu.HBM)
    dma = pltpu.SemaphoreType.DMA
    shapes = ((rows, width), (text_rows, width), (block, width))
    held = pl.pallas_call(
        functools.partial(kernel, n_txt, n_aud),
        out_shape=tuple(pltpu.VMEM(shape, f32) for shape in shapes),
        in_specs=[anywhere] * 7,
        out_specs=(vmem,) * 3,
        scratch_shapes=[
            pltpu.VMEM((1, rows), jnp.int32),
            pltpu.VMEM((1, rows), jnp.int32),
            pltpu.SMEM((1,), f32),
            pltpu.SMEM((1,), f32),
            pltpu.VMEM((rows, width), f32),
            pltpu.VMEM((rows, width), bf16),
            pltpu.VMEM((n_txt, 2, text_rows // 2, width), f32),
            pltpu.VMEM((HOPS + 1, block, width), f32),
            pltpu.VMEM((n_txt * cols, width), bf16),
            pltpu.VMEM((n_txt * cols, rows), bf16),
            pltpu.VMEM((slots, 8, width), f32),
            pltpu.VMEM((n_txt, n_aud) + chunk, f32),
            pltpu.VMEM((n_txt, n_aud) + chunk, f32),
            pltpu.VMEM((n_txt,) + chunk, f32),
            pltpu.VMEM((n_txt,) + chunk, f32),
            pltpu.VMEM(chunk, f32),
            pltpu.VMEM((n_aud,) + chunk, f32),
            pltpu.VMEM((HOPS + 1, block, width), f32),
            pltpu.VMEM((HOPS + 1, block, width), f32),
            pltpu.VMEM((block, width), f32),
            pltpu.VMEM((n_txt, block, width), f32),
            dma((8,)),
            dma((n_txt,)),
            dma((n_txt,)),
            dma((n_txt,)),
            dma((n_txt,)),
            dma((HOPS + 1,)),
            dma((HOPS + 1,)),
            dma,
            dma((n_txt,)),
            dma((HOPS + 1,)),
            dma((HOPS + 1,)),
            dma((n_txt,)),
            dma((n_txt,)),
            dma((n_txt,)),
            dma((n_txt,)),
            dma((n_aud,)),
            dma((n_aud,)),
        ],
        compiler_params=pltpu.CompilerParams(
            collective_id=0, has_side_effects=True, vmem_limit_bytes=56 * 1024 * 1024
        ),
        name="trilinear",
    )(
        images,
        texts,
        audio,
        pos_text.reshape(1, rows),
        pos_audio.reshape(1, rows),
        logit_scale,
        logit_bias,
    )
    return pl.pallas_call(
        put_out,
        out_shape=tuple(jax.ShapeDtypeStruct(shape, f32) for shape in shapes),
        in_specs=[vmem] * 3,
        out_specs=(anywhere,) * 3,
        scratch_shapes=[dma((3,))],
        name="put_out",
    )(*[pltpu.with_memory_space_constraint(h, pltpu.VMEM) for h in held])


def solution(mesh):
    placed = (
        P(("txt", "aud"), None),
        P("txt", None),
        P("aud", None),
        P(("txt", "aud")),
        P(("txt", "aud")),
        P(),
        P(),
    )
    return jax.shard_map(
        functools.partial(shards, mesh.shape["txt"], mesh.shape["aud"]),
        mesh=mesh,
        in_specs=placed,
        out_specs=(P(("txt", "aud"), None), P("txt", None), P("aud", None)),
        check_vma=False,
    )
```
